32 devices in a mesh: row: 8 (over y, x, core), col: 4 (over z).
Axes of the slice: x: 2, y: 2, z: 4, core: 2. Of those that a mesh axis runs over, the one named last changes fastest.
Arguments:
- design: bfloat16 [512, 90112], P(('row', 'col')), may hold values from -6 to 6
- arc_partials: float32 [32, 6, 16], P(('row', 'col')), may hold values from -6 to 6
- arc_id: int32 [32], P(('row', 'col')), may hold values from 0 to 7
- arc_weight: float32 [8], replicated, may hold values from 0.25 to 4
Outputs:
- normal_slab: float32 [90112, 2048], P('row', 'col')
The draws below stay inside these ranges and needn't reach their ends.
All inputs are finite; a program needn't handle non-finite values.
Results may differ from the reference program's by a relative error of at most 0.0003.
The reference program's roundings to bfloat16 on the way count: a program that leaves them out, or rounds other values in their place, can miss the bound.
Values may be sent and summed in bfloat16 or wider, within the bound.
A program may use at most 128 MiB of HBM per device.

```python
import math
import jax
import jax.numpy as jnp
from jax import lax

K = 90112
SLAB = 2048
E_DEV = 16
PARAMS = 6
ARCS = 8
SEGMENTS = 32
EPOCHS = 512


def with_ends(values, key, smallest, top_value):
    dims = values.shape
    place = [jax.random.randint(jax.random.fold_in(key, axis), (), 0, dims[axis]) for axis in range(len(dims))]
    values = values.at[tuple(place)].set(smallest)
    longest = dims.index(max(dims))
    place[longest] = (place[longest] + 1) % dims[longest]
    return values.at[tuple(place)].set(top_value)


def block_levels(key, extent, shards, low, top_value):
    level, own = 1.0, jax.random.fold_in(key, 6)
    for dim, shards_of in shards:
        steps = jnp.exp(jax.random.uniform(jax.random.fold_in(own, dim), (shards_of,), jnp.float32, low / len(shards), top_value / len(shards)))
        level = level * jnp.repeat(steps, extent[dim] // shards_of).reshape([-1 if axis == dim else 1 for axis in range(len(extent))])
    return level


def gaussian(key, shape, scale, bound, cuts=(), kind=jnp.bfloat16):
    drawn = jax.random.normal(key, shape, jnp.float32) * scale
    if len(cuts) > 0:
        drawn = block_levels(key, shape, cuts, -0.22, 0.18) * drawn
    return jnp.clip(drawn, min=-bound, max=bound).astype(kind)


def setup_inputs(seed: int = 0) -> dict:
    splits = jax.random.split(jax.random.key(seed), 5)
    design = gaussian(splits[0], (EPOCHS, K), 1.0, 6.0, ((0, 32),))
    arc_partials = gaussian(splits[1], (SEGMENTS, PARAMS, E_DEV), 1.0, 6.0, ((0, 32),), jnp.float32)
    arc_id = with_ends(jax.random.randint(splits[2], (SEGMENTS,), 0, ARCS), jax.random.fold_in(splits[2], 1), 0, ARCS - 1).astype(jnp.int32)
    arc_weight = jnp.clip(jnp.exp(jax.random.uniform(splits[3], (ARCS,), jnp.float32, math.log(0.25), math.log(4.0))), 0.25, 4.0)
    return dict(design=design, arc_partials=arc_partials, arc_id=arc_id, arc_weight=arc_weight)


ridge = 4.0


def solve_small(matrix, rhs):
    order = matrix.shape[-1]
    for pivot in range(order):
        scale = 1.0 / matrix[..., pivot, pivot]
        row_mat = matrix[..., pivot, :] * scale[..., None]
        row_rhs = rhs[..., pivot, :] * scale[..., None]
        factor = matrix[..., :, pivot]
        matrix = matrix - factor[..., :, None] * row_mat[..., None, :]
        rhs = rhs - factor[..., :, None] * row_rhs[..., None, :]
        matrix = matrix.at[..., pivot, :].set(row_mat)
        rhs = rhs.at[..., pivot, :].set(row_rhs)
    return rhs


def reference(design, arc_partials, arc_id, arc_weight):
    high = lax.Precision.HIGHEST
    segments = arc_partials.shape[0]
    slab_rows = design[:, :SLAB].astype(jnp.float32).reshape(segments, E_DEV, SLAB)
    coupling = jnp.einsum("npe,nes->nps", arc_partials, slab_rows, precision=high)
    gram = jnp.einsum("npe,nqe->npq", arc_partials, arc_partials, precision=high)
    arc_gram = jax.ops.segment_sum(gram, arc_id, ARCS)
    arc_coupling = jax.ops.segment_sum(coupling, arc_id, ARCS)
    own_gram = arc_gram[arc_id] + ridge * jnp.eye(PARAMS, dtype=jnp.float32)
    solved = solve_small(own_gram, arc_coupling[arc_id])
    reduced = slab_rows - jnp.einsum("npe,nps->nes", arc_partials, solved, precision=high)
    weights = arc_weight[arc_id]
    eliminated = (weights[:, None, None] * reduced).astype(jnp.bfloat16).reshape(EPOCHS, SLAB)
    product = jnp.dot(design.astype(jnp.float32).T, eliminated.astype(jnp.float32), precision=high, preferred_element_type=jnp.float32)
    return product * (1.0 / EPOCHS)
```

```python
import functools

import jax
import jax.numpy as jnp
from jax import lax
from jax.experimental import pallas as pl
from jax.experimental.pallas import tpu as pltpu
from jax.sharding import PartitionSpec as P

SLAB = 2048
SHARES = (4, 12, 6)


ridge = 4.0


def solve_small(matrix, rhs):
    order = matrix.shape[-1]
    for pivot in range(order):
        scale = 1.0 / matrix[..., pivot, pivot]
        row_mat = matrix[..., pivot, :] * scale[..., None]
        row_rhs = rhs[..., pivot, :] * scale[..., None]
        factor = matrix[..., :, pivot]
        matrix = matrix - factor[..., :, None] * row_mat[..., None, :]
        rhs = rhs - factor[..., :, None] * row_rhs[..., None, :]
        matrix = matrix.at[..., pivot, :].set(row_mat)
        rhs = rhs.at[..., pivot, :].set(row_rhs)
    return rhs


def after(value, token):
    return lax.optimization_barrier((value, token))[0]


def eliminated_columns(slab, partials, ids, arc_weight):
    high = lax.Precision.HIGHEST
    segments, order, rows_dev = partials.shape
    arcs = arc_weight.shape[0]
    select = (jnp.arange(arcs)[:, None] == ids[None, :]).astype(jnp.float32)
    gram = jnp.einsum("npe,nqe->npq", partials, partials, precision=high)
    arc_gram = jnp.einsum("an,npq->apq", select, gram, precision=high)
    arc_gram = arc_gram + ridge * jnp.eye(order, dtype=jnp.float32)
    spread = select[:, None, :, None] * partials.transpose(1, 0, 2)[None]
    spread = spread.reshape(arcs * order, segments * rows_dev)
    values = slab.astype(jnp.float32)
    coupling = jnp.dot(spread, values, precision=high, preferred_element_type=jnp.float32)
    solved = solve_small(arc_gram, coupling.reshape(arcs, order, -1))
    fitted = lax.dot_general(
        spread,
        solved.reshape(arcs * order, -1),
        (((0,), (0,)), ((), ())),
        precision=high,
        preferred_element_type=jnp.float32,
    )
    weights = jnp.repeat(jnp.sum(select * arc_weight[:, None], axis=0), rows_dev)
    return (weights[:, None] * (values - fitted)).astype(jnp.bfloat16)


def product_kernel(scale, piece_ref, slab_ref, *rest):
    out_ref = rest[-1]
    out_ref[...] = scale * lax.dot_general(
        piece_ref[...],
        slab_ref[...],
        (((0,), (0,)), ((), ())),
        preferred_element_type=jnp.float32,
    )


def product_into(total, piece, ordered, first, tile, rows, scale):
    epochs, width = piece.shape
    columns = ordered.shape[1]
    operands = [piece, ordered]
    in_specs = [
        pl.BlockSpec((epochs, tile), lambda i: (0, i)),
        pl.BlockSpec((epochs, columns), lambda i: (0, 0)),
    ]
    aliases = {}
    if total is not None:
        operands.append(total)
        in_specs.append(pl.BlockSpec(memory_space=pl.ANY))
        aliases = {2: 0}
    return pl.pallas_call(
        functools.partial(product_kernel, scale),
        out_shape=jax.ShapeDtypeStruct((rows, columns), jnp.float32),
        grid=(width // tile,),
        in_specs=in_specs,
        out_specs=pl.BlockSpec((tile, columns), lambda i: (first // tile + i, 0)),
        input_output_aliases=aliases,
        compiler_params=pltpu.CompilerParams(vmem_limit_bytes=40 << 20),
        cost_estimate=pl.CostEstimate(
            flops=2 * epochs * width * columns,
            bytes_accessed=2 * epochs * (width + columns) + 4 * width * columns,
            transcendentals=0,
        ),
    )(*operands)


def cuts(rows):
    tile = next(t for t in (512, 256, 128) if rows % t == 0)
    tiles, ends, seen = rows // tile, [], 0
    for share in SHARES:
        seen += share
        ends.append(tiles * seen // sum(SHARES) * tile)
    starts = [0] + ends[:-1]
    return tile, [(a, b - a) for a, b in zip(starts, ends) if b > a]


def local(design, arc_partials, arc_id, arc_weight):
    rows_dev, coefficients = design.shape
    row_count = lax.axis_size("row")
    col_count = lax.axis_size("col")
    devices = row_count * col_count
    epochs = rows_dev * devices
    rows = coefficients // row_count
    order = arc_partials.shape[1]
    tile, pieces = cuts(rows)
    split = design.reshape(rows_dev, row_count, rows)

    gathered, token = [], None
    ordered = None
    for number, (first, width) in enumerate(pieces):
        source = split[:, :, first : first + width]
        if token is not None:
            source = after(source, token)
        source = source.transpose(1, 0, 2)
        own = lax.all_to_all(source, "row", split_axis=0, concat_axis=0, tiled=True)
        token = own
        gathered.append(
            lax.all_gather(own.reshape(row_count * rows_dev, width), "col", axis=0, tiled=True)
        )
        if number == 1:
            slab_own = after(design[:, :SLAB], token)
            columns = lax.all_to_all(slab_own, "col", split_axis=1, concat_axis=0, tiled=True)
            facts = jnp.concatenate(
                [arc_partials.reshape(1, -1), arc_id.astype(jnp.float32)[:, None]], axis=1
            )
            width_facts = facts.shape[1]
            facts = jnp.broadcast_to(after(facts, columns), (devices, width_facts))
            facts = lax.all_to_all(facts, ("row", "col"), split_axis=0, concat_axis=0, tiled=True)
            spread = jnp.broadcast_to(
                after(columns, facts)[None], (row_count,) + columns.shape
            )
            slab = lax.all_to_all(spread, "row", split_axis=0, concat_axis=0, tiled=True)
            token = slab
            slab = slab.reshape(epochs, columns.shape[1])
            partials = facts[:, :-1].reshape(devices, order, rows_dev)
            ids = facts[:, -1].astype(jnp.int32)
            eliminated = eliminated_columns(slab, partials, ids, arc_weight)
            ordered = eliminated.reshape(row_count, col_count, rows_dev, -1)
            ordered = ordered.transpose(1, 0, 2, 3).reshape(epochs, -1)

    total = None
    for (first, width), piece in zip(pieces, gathered):
        total = product_into(total, piece, ordered, first, tile, rows, 1.0 / epochs)
    return total


def solution(mesh):
    placed = (P(("row", "col"), None), P(("row", "col"), None, None), P(("row", "col")), P())
    return jax.shard_map(
        local, mesh=mesh, in_specs=placed, out_specs=P("row", "col"), check_vma=False
    )
```

```python
import functools

import jax
import jax.numpy as jnp
from jax import lax
from jax.experimental import pallas as pl
from jax.experimental.pallas import tpu as pltpu
from jax.sharding import PartitionSpec as P

SLAB = 2048
SHARES = (12, 10)


ridge = 4.0


def solve_small(matrix, rhs):
    order = matrix.shape[-1]
    for pivot in range(order):
        scale = 1.0 / matrix[..., pivot, pivot]
        row_mat = matrix[..., pivot, :] * scale[..., None]
        row_rhs = rhs[..., pivot, :] * scale[..., None]
        factor = matrix[..., :, pivot]
        matrix = matrix - factor[..., :, None] * row_mat[..., None, :]
        rhs = rhs - factor[..., :, None] * row_rhs[..., None, :]
        matrix = matrix.at[..., pivot, :].set(row_mat)
        rhs = rhs.at[..., pivot, :].set(row_rhs)
    return rhs


def after(value, token):
    return lax.optimization_barrier((value, token))[0]


def eliminated_columns(slab, partials, ids, arc_weight):
    high = lax.Precision.HIGHEST
    segments, order, rows_dev = partials.shape
    arcs = arc_weight.shape[0]
    select = (jnp.arange(arcs)[:, None] == ids[None, :]).astype(jnp.float32)
    gram = jnp.einsum("npe,nqe->npq", partials, partials, precision=high)
    arc_gram = jnp.einsum("an,npq->apq", select, gram, precision=high)
    arc_gram = arc_gram + ridge * jnp.eye(order, dtype=jnp.float32)
    spread = select[:, None, :, None] * partials.transpose(1, 0, 2)[None]
    spread = spread.reshape(arcs * order, segments * rows_dev)
    values = slab.astype(jnp.float32)
    coupling = jnp.dot(spread, values, precision=high, preferred_element_type=jnp.float32)
    solved = solve_small(arc_gram, coupling.reshape(arcs, order, -1))
    fitted = lax.dot_general(
        spread,
        solved.reshape(arcs * order, -1),
        (((0,), (0,)), ((), ())),
        precision=high,
        preferred_element_type=jnp.float32,
    )
    weights = jnp.repeat(jnp.sum(select * arc_weight[:, None], axis=0), rows_dev)
    return (weights[:, None] * (values - fitted)).astype(jnp.bfloat16)


def product_kernel(scale, piece_ref, slab_ref, *rest):
    out_ref = rest[-1]
    out_ref[...] = scale * lax.dot_general(
        piece_ref[...],
        slab_ref[...],
        (((0,), (0,)), ((), ())),
        preferred_element_type=jnp.float32,
    )


def product_into(total, piece, ordered, first, tile, rows, scale):
    epochs, width = piece.shape
    columns = ordered.shape[1]
    operands = [piece, ordered]
    in_specs = [
        pl.BlockSpec((epochs, tile), lambda i: (0, i)),
        pl.BlockSpec((epochs, columns), lambda i: (0, 0)),
    ]
    aliases = {}
    if total is not None:
        operands.append(total)
        in_specs.append(pl.BlockSpec(memory_space=pl.ANY))
        aliases = {2: 0}
    return pl.pallas_call(
        functools.partial(product_kernel, scale),
        out_shape=jax.ShapeDtypeStruct((rows, columns), jnp.float32),
        grid=(width // tile,),
        in_specs=in_specs,
        out_specs=pl.BlockSpec((tile, columns), lambda i: (first // tile + i, 0)),
        input_output_aliases=aliases,
        compiler_params=pltpu.CompilerParams(vmem_limit_bytes=40 << 20),
        cost_estimate=pl.CostEstimate(
            flops=2 * epochs * width * columns,
            bytes_accessed=2 * epochs * (width + columns) + 4 * width * columns,
            transcendentals=0,
        ),
    )(*operands)


def cuts(rows):
    tile = next(t for t in (512, 256, 128) if rows % t == 0)
    tiles, ends, seen = rows // tile, [], 0
    for share in SHARES:
        seen += share
        ends.append(tiles * seen // sum(SHARES) * tile)
    starts = [0] + ends[:-1]
    return tile, [(a, b - a) for a, b in zip(starts, ends) if b > a]


def local(design, arc_partials, arc_id, arc_weight):
    rows_dev, coefficients = design.shape
    row_count = lax.axis_size("row")
    col_count = lax.axis_size("col")
    devices = row_count * col_count
    epochs = rows_dev * devices
    rows = coefficients // row_count
    order = arc_partials.shape[1]
    tile, pieces = cuts(rows)
    split = design.reshape(rows_dev, row_count, rows)

    first, width = pieces[0]
    whole = lax.all_gather(split[:, :, first : first + width], "col", axis=0, tiled=True)

    gathered, token = [], None
    for first, width in pieces[1:]:
        source = split[:, :, first : first + width]
        if token is not None:
            source = after(source, token)
        own = lax.all_to_all(
            source.transpose(1, 0, 2), "row", split_axis=0, concat_axis=0, tiled=True
        )
        token = own
        gathered.append(
            lax.all_gather(own.reshape(row_count * rows_dev, -1), "col", axis=0, tiled=True)
        )

    slab_own = design[:, :SLAB]
    if token is not None:
        slab_own = after(slab_own, token)
    columns = lax.all_to_all(slab_own, "col", split_axis=1, concat_axis=0, tiled=True)
    facts = jnp.concatenate(
        [arc_partials.reshape(1, -1), arc_id.astype(jnp.float32)[:, None]], axis=1
    )
    facts = jnp.broadcast_to(after(facts, columns), (devices, facts.shape[1]))
    facts = lax.all_to_all(facts, ("row", "col"), split_axis=0, concat_axis=0, tiled=True)
    spread = jnp.broadcast_to(after(columns, facts)[None], (row_count,) + columns.shape)
    slab = lax.all_to_all(spread, "row", split_axis=0, concat_axis=0, tiled=True)
    partials = facts[:, :-1].reshape(devices, order, rows_dev)
    ids = facts[:, -1].astype(jnp.int32)
    eliminated = eliminated_columns(slab.reshape(epochs, -1), partials, ids, arc_weight)
    ordered = eliminated.reshape(row_count, col_count, rows_dev, -1)
    ordered = ordered.transpose(1, 0, 2, 3).reshape(epochs, -1)

    dealt = lax.all_to_all(
        after(whole, eliminated).transpose(1, 0, 2), "row", split_axis=0, concat_axis=0, tiled=True
    )
    scale = 1.0 / epochs
    total = product_into(
        None, dealt.reshape(epochs, -1), eliminated, pieces[0][0], tile, rows, scale
    )
    for (first, width), piece in zip(pieces[1:], gathered):
        total = product_into(total, piece, ordered, first, tile, rows, scale)
    return total


def solution(mesh):
    placed = (P(("row", "col"), None), P(("row", "col"), None, None), P(("row", "col")), P())
    return jax.shard_map(
        local, mesh=mesh, in_specs=placed, out_specs=P("row", "col"), check_vma=False
    )
```
